32 devices in a mesh: seq: 4 (over x, core), chan: 8 (over z, y).
Axes of the slice: x: 2, y: 2, z: 4, core: 2. Of those that a mesh axis runs over, the one named last changes fastest.
Arguments:
- signal_in: bfloat16 [1024, 8192], P('seq', 'chan'), may hold values from -6 to 6
- gate_in: bfloat16 [1024, 8192], P('seq', 'chan'), may hold values from -6 to 6
- outer_gate: bfloat16 [1024, 8192], P('seq', 'chan'), may hold values from -6 to 6
- cotangent: bfloat16 [1024, 8192], P('seq', 'chan'), may hold values from -6 to 6
- residues: float32 [16, 512], replicated, may hold values from -4 to 4
- log_rates: float32 [16, 512], replicated, may hold values from -11 to -2.5
Outputs:
- grad_signal: bfloat16 [1024, 8192], P('seq', 'chan')
- grad_gate: bfloat16 [1024, 8192], P('seq', 'chan')
- grad_outer: bfloat16 [1024, 8192], P('seq', 'chan')
- grad_residues: float32 [16, 512], replicated
- grad_log_rates: float32 [16, 512], replicated
The draws below stay inside these ranges and needn't reach their ends.
All inputs are finite; a program needn't handle non-finite values.
Results may differ from the reference program's by a relative error of at most 0.01.
Values may be sent and summed in bfloat16 or wider, within the bound.
A program may use at most 64 MiB of HBM per device.

```python
import math
import jax
import jax.numpy as jnp
from jax import lax

D = 8192
FILTERS = 512
MODES = 16
TOKENS = 1024


def block_scale(key, dims, cuts, least, top_value):
    loudness = 1.0
    for position, blocks in cuts:
        steps = jax.random.uniform(jax.random.fold_in(jax.random.fold_in(key, 6), position), (blocks,), jnp.float32, least / len(cuts), top_value / len(cuts))
        loudness = loudness * jnp.repeat(jnp.exp(steps), dims[position] // blocks).reshape((-1,) + (1,) * (len(dims) - 1 - position))
    return loudness


def bell_draw(key, shape, deviation, reach, cuts=(), dtype=jnp.bfloat16):
    values = jax.random.normal(key, shape, jnp.float32) * deviation
    if len(cuts) > 0:
        values = block_scale(key, shape, cuts, -0.22, 0.18) * values
    return jnp.clip(values, min=-reach, max=reach).astype(dtype)


def setup_inputs(seed: int = 0) -> dict:
    arg_keys = jax.random.split(jax.random.key(seed), 7)
    signal_in = bell_draw(arg_keys[0], (TOKENS, D), 1.0, 6.0, ((0, 4), (1, 8)))
    gate_in = bell_draw(arg_keys[1], (TOKENS, D), 1.0, 6.0, ((0, 4), (1, 8)))
    outer_gate = bell_draw(arg_keys[2], (TOKENS, D), 1.0, 6.0, ((0, 4), (1, 8)))
    cotangent = bell_draw(arg_keys[3], (TOKENS, D), 1.0, 6.0, ((0, 4), (1, 8)))
    residues = bell_draw(arg_keys[4], (MODES, FILTERS), 0.6, 4.0, (), jnp.float32)
    log_rates = jnp.clip(jax.random.uniform(arg_keys[5], (MODES, FILTERS), jnp.float32, -11.0, -2.5), -11.0, -2.5)
    return dict(signal_in=signal_in, gate_in=gate_in, outer_gate=outer_gate, cotangent=cotangent, residues=residues, log_rates=log_rates)


def reference(signal_in, gate_in, outer_gate, cotangent, residues, log_rates):
    width = math.gcd(FILTERS, 256)
    count = D // width
    period = 2 * TOKENS
    scale = TOKENS ** -0.5
    norm = (TOKENS * D // FILTERS) ** -0.5
    times = jnp.arange(TOKENS).astype(jnp.float32)

    def columns(array, start):
        return lax.dynamic_slice_in_dim(array, start, width, 1).astype(jnp.float32)

    def one_block(carry, index):
        start = index * width
        offset = start % FILTERS
        signal = columns(signal_in, start)
        gate = columns(gate_in, start)
        outer = columns(outer_gate, start)
        upstream = columns(cotangent, start)
        residue_columns = lax.dynamic_slice_in_dim(residues, offset, width, 1)
        rate = jnp.exp(lax.dynamic_slice_in_dim(log_rates, offset, width, 1))
        basis = jnp.exp(-rate[None] * times[:, None, None])
        impulse = scale * jnp.sum(residue_columns[None] * basis, 1)
        gated = lax.optimization_barrier((signal * gate).astype(jnp.bfloat16)).astype(jnp.float32)
        weighted = lax.optimization_barrier((upstream * outer).astype(jnp.bfloat16)).astype(jnp.float32)
        spectrum_gated = jnp.fft.rfft(gated, n=period, axis=0)
        spectrum_weighted = jnp.fft.rfft(weighted, n=period, axis=0)
        spectrum_impulse = jnp.fft.rfft(impulse, n=period, axis=0)
        convolved = jnp.fft.irfft(spectrum_gated * spectrum_impulse, n=period, axis=0)[:TOKENS]
        grad_gated = jnp.fft.irfft(spectrum_weighted * jnp.conj(spectrum_impulse), n=period, axis=0)[:TOKENS]
        lag_grad = jnp.fft.irfft(spectrum_weighted * jnp.conj(spectrum_gated), n=period, axis=0)[:TOKENS]
        moment = lag_grad[:, None, :] * basis
        first = scale * jnp.sum(moment, 0)
        second = -scale * residue_columns * rate * jnp.sum(moment * times[:, None, None], 0)
        total_first = lax.dynamic_update_slice_in_dim(carry[0], lax.dynamic_slice_in_dim(carry[0], offset, width, 1) + first, offset, 1)
        total_second = lax.dynamic_update_slice_in_dim(carry[1], lax.dynamic_slice_in_dim(carry[1], offset, width, 1) + second, offset, 1)
        outputs = ((grad_gated * gate).astype(jnp.bfloat16), (grad_gated * signal).astype(jnp.bfloat16), (upstream * convolved).astype(jnp.bfloat16))
        return (total_first, total_second), outputs

    zeros = jnp.zeros((MODES, FILTERS), jnp.float32)
    totals, pieces = lax.scan(one_block, (zeros, zeros), jnp.arange(count).astype(jnp.int32))

    def unblock(stacked):
        return jnp.transpose(stacked, (1, 0, 2)).reshape(TOKENS, D)

    return unblock(pieces[0]), unblock(pieces[1]), unblock(pieces[2]), norm * totals[0], norm * totals[1]
```

```python
import functools
import math

import jax
import jax.numpy as jnp
from jax import lax
from jax.experimental import pallas as pl
from jax.experimental.pallas import tpu as pltpu
from jax.sharding import PartitionSpec as P

LANES = 128
SUB = 8
SEG = 16
f32 = jnp.float32


def rows_of(ref, first, stride):
    return ref[pl.ds(first, SUB, stride=stride), :]


def spread(ref, row):
    return jnp.broadcast_to(ref[pl.ds(row, 1), :], (SUB, LANES))


def filter_lanes(block, cols, filters):
    start = lax.axis_index("chan") * cols + block * LANES
    return pl.ds(pl.multiple_of(lax.rem(start, filters), LANES), LANES)


def block_lanes(block):
    return pl.ds(pl.multiple_of(block * LANES, LANES), LANES)


def local_phase(
    scale, sig, gate, outer, cot, res, logr, conv, grad, xs, ys, edge, moment, gsum,
    g_s, w_s, a_s, h_s, pw_s, c_s, d_s, st, lag_s,
):
    rows, cols = sig.shape
    modes, filters = res.shape
    segs = rows // SEG
    groups = segs // SUB

    @pl.loop(0, cols // LANES)
    def _(block):
        lanes = block_lanes(block)
        fl = filter_lanes(block, cols, filters)
        g_s[...] = (sig[:, lanes].astype(f32) * gate[:, lanes].astype(f32)).astype(jnp.bfloat16).astype(f32)
        w_s[...] = (cot[:, lanes].astype(f32) * outer[:, lanes].astype(f32)).astype(jnp.bfloat16).astype(f32)
        rate = jnp.exp(logr[:, fl])
        amp = res[:, fl] * scale
        a = jnp.exp(-rate)
        a_s[...] = a
        power = jnp.ones((modes, LANES), f32)
        for u in range(SEG):
            pw_s[u * modes : (u + 1) * modes, :] = power
            h_s[u : u + 1, :] = jnp.sum(amp * power, 0, keepdims=True)
            power = power * a
        seg_decay = power

        @pl.loop(0, groups)
        def _(group):
            base = group * (SUB * SEG)
            for half in range(0, modes, SUB):
                decay = [spread(a_s, half + k) for k in range(SUB)]
                zero = jnp.zeros((SUB, LANES), f32)
                x, z, y, v = ([zero] * SUB for _ in range(4))
                for j in range(SEG):
                    gj = rows_of(g_s, base + j, SEG)
                    wj = rows_of(w_s, base + SEG - 1 - j, SEG)
                    for k in range(SUB):
                        x[k] = decay[k] * (x[k] + gj)
                        z[k] = decay[k] * z[k] + x[k]
                        t = decay[k] * y[k]
                        y[k] = t + wj
                        v[k] = decay[k] * v[k] + t
                for k in range(SUB):
                    at = pl.ds(pl.multiple_of((half + k) * segs + group * SUB, SUB), SUB)
                    st[0, at, :] = x[k]
                    st[1, at, :] = z[k]
                    st[2, at, :] = y[k]
                    st[3, at, :] = v[k]
            g = [rows_of(g_s, base + j, SEG) for j in range(SEG)]
            w = [rows_of(w_s, base + j, SEG) for j in range(SEG)]
            for u in range(SEG):
                total = w[u] * g[0]
                for j in range(u + 1, SEG):
                    total = total + w[j] * g[j - u]
                lag_s[pl.ds(pl.multiple_of((group * SEG + u) * SUB, SUB), SUB), :] = total
            h = [spread(h_s, u) for u in range(SEG)]
            for j in range(SEG):
                forward = h[0] * g[j]
                for u in range(1, j + 1):
                    forward = forward + h[u] * g[j - u]
                c_s[pl.ds(base + j, SUB, stride=SEG), :] = forward
                backward = h[0] * w[j]
                for u in range(1, SEG - j):
                    backward = backward + h[u] * w[j + u]
                d_s[pl.ds(base + j, SUB, stride=SEG), :] = backward

        conv[:, lanes] = c_s[...]
        grad[:, lanes] = d_s[...]

        gr = jnp.zeros((modes, LANES), f32)
        gl = jnp.zeros((modes, LANES), f32)
        for u in range(SEG):
            total = lag_s[u * SUB : (u + 1) * SUB, :]
            for group in range(1, groups):
                first = (group * SEG + u) * SUB
                total = total + lag_s[first : first + SUB, :]
            term = jnp.sum(total, 0, keepdims=True) * pw_s[u * modes : (u + 1) * modes, :]
            gr = gr + term
            if u > 0:
                gl = gl + float(u) * term
        x = jnp.zeros((modes, LANES), f32)
        xd = x
        for seg in range(segs):
            at = pl.ds(seg, modes, stride=segs)
            e, d, y, v = (st[i, at, :] for i in range(4))
            xs[seg * modes : (seg + 1) * modes, lanes] = x
            if seg > 0:
                gr = gr + x * y
                gl = gl + (xd * y + x * v)
            xd = seg_decay * (xd + float(SEG) * x) + d
            x = seg_decay * x + e
        y = jnp.zeros((modes, LANES), f32)
        yv = y
        for seg in reversed(range(segs)):
            at = pl.ds(seg, modes, stride=segs)
            ys[seg * modes : (seg + 1) * modes, lanes] = y
            yv = st[3, at, :] + seg_decay * (yv + float(SEG) * y)
            y = st[2, at, :] + seg_decay * y
        edge[0, :, lanes] = x
        edge[1, :, lanes] = y
        moment[0, :, lanes] = xd
        moment[1, :, lanes] = yv
        gsum[0, :, lanes] = gr
        gsum[1, :, lanes] = gl


def carried(edges, parts, span, rate, fl_lanes):
    place = lax.axis_index("seq")
    shape = rate.shape
    x0 = jnp.zeros(shape, f32)
    xm = jnp.zeros(shape, f32)
    y0 = jnp.zeros(shape, f32)
    for other in range(parts):
        ahead = jnp.maximum(place - 1 - other, 0).astype(f32) * float(span)
        behind = jnp.maximum(other - place - 1, 0).astype(f32) * float(span)
        e = jnp.where(other < place, edges[other, 0, :, fl_lanes].astype(f32), 0.0) * jnp.exp(-rate * ahead)
        x0 = x0 + e
        xm = xm + ahead * e
        y0 = y0 + jnp.where(other > place, edges[other, 1, :, fl_lanes].astype(f32), 0.0) * jnp.exp(-rate * behind)
    return x0, xm, y0


def gradient_phase(scale, parts, span, edges, edge, moment, gsum, res, logr, totals, carry):
    modes, filters = res.shape
    cols = edge.shape[2]
    totals[...] = jnp.zeros_like(totals)

    @pl.loop(0, cols // LANES)
    def _(block):
        lanes = block_lanes(block)
        fl = filter_lanes(block, cols, filters)
        rate = jnp.exp(logr[:, fl])
        x0, xm, y0 = carried(edges, parts, span, rate, lanes)
        carry[0, :, lanes] = x0
        carry[1, :, lanes] = y0
        w = edge[1, :, lanes]
        gr = gsum[0, :, lanes] + x0 * w
        gl = gsum[1, :, lanes] + x0 * moment[1, :, lanes] + xm * w + moment[0, :, lanes] * y0
        totals[0, :, fl] = totals[0, :, fl] + scale * gr
        totals[1, :, fl] = totals[1, :, fl] - scale * (res[:, fl] * rate) * gl


def output_phase(
    scale, sig, gate, cot, res, logr, conv, grad, xs, ys, carry, out_sig, out_gate, out_outer,
    a_s, c_s, d_s, p_s, q_s,
):
    rows, cols = sig.shape
    modes, filters = res.shape
    segs = rows // SEG
    groups = segs // SUB

    @pl.loop(0, cols // LANES)
    def _(block):
        lanes = block_lanes(block)
        fl = filter_lanes(block, cols, filters)
        rate = jnp.exp(logr[:, fl])
        amp = res[:, fl] * scale
        a_s[...] = jnp.exp(-rate)
        seg_decay = jnp.exp(-rate * float(SEG))
        p = amp * carry[0, :, lanes]
        q = amp * carry[1, :, lanes]
        for seg in range(segs):
            at = slice(seg * modes, (seg + 1) * modes)
            p_s[at, :] = amp * xs[at, lanes] + p
            p = p * seg_decay
            back = segs - 1 - seg
            at = slice(back * modes, (back + 1) * modes)
            q_s[at, :] = amp * ys[at, lanes] + q
            q = q * seg_decay
        c_s[...] = conv[:, lanes]
        d_s[...] = grad[:, lanes]

        @pl.loop(0, groups)
        def _(group):
            base = group * (SUB * SEG)
            for half in range(0, modes, SUB):
                decay = [spread(a_s, half + k) for k in range(SUB)]
                p = [rows_of(p_s, group * (SUB * modes) + half + k, modes) for k in range(SUB)]
                q = [rows_of(q_s, group * (SUB * modes) + half + k, modes) for k in range(SUB)]
                for j in range(SEG):
                    at = pl.ds(base + j, SUB, stride=SEG)
                    c_s[at, :] = c_s[at, :] + tree(p)
                    q = [decay[k] * q[k] for k in range(SUB)]
                    at = pl.ds(base + SEG - 1 - j, SUB, stride=SEG)
                    d_s[at, :] = d_s[at, :] + tree(q)
                    if j < SEG - 1:
                        p = [decay[k] * p[k] for k in range(SUB)]

        d = d_s[...]
        out_sig[:, lanes] = (d * gate[:, lanes].astype(f32)).astype(jnp.bfloat16)
        out_gate[:, lanes] = (d * sig[:, lanes].astype(f32)).astype(jnp.bfloat16)
        out_outer[:, lanes] = (c_s[...] * cot[:, lanes].astype(f32)).astype(jnp.bfloat16)


def tree(values):
    while len(values) > 1:
        values = [values[i] + values[i + 1] for i in range(0, len(values), 2)]
    return values[0]


def finish_phase(scale, parts, span, sig, gate, cot, res, logr, conv, grad, xs, ys, edges, edge, moment, gsum,
                 out_sig, out_gate, out_outer, totals, carry, a_s, c_s, d_s, p_s, q_s):
    gradient_phase(scale, parts, span, edges, edge, moment, gsum, res, logr, totals, carry)
    output_phase(scale, sig, gate, cot, res, logr, conv, grad, xs, ys, carry, out_sig, out_gate, out_outer,
                 a_s, c_s, d_s, p_s, q_s)


def on_device(signal_in, gate_in, outer_gate, cotangent, residues, log_rates):
    parts = lax.axis_size("seq")
    rows, cols = signal_in.shape
    modes, filters = residues.shape
    total = parts * rows
    width = cols * lax.axis_size("chan")
    segs = rows // SEG
    groups = segs // SUB
    scale = float(total) ** (-0.5)
    norm = float(total * width // filters) ** (-0.5)
    whole = pl.BlockSpec(memory_space=pltpu.VMEM)
    shape = jax.ShapeDtypeStruct
    params = pltpu.CompilerParams(vmem_limit_bytes=48 * 1024 * 1024)
    tile = pltpu.VMEM((rows, LANES), f32)
    conv, grad, xs, ys, edge, moment, gsum = pl.pallas_call(
        functools.partial(local_phase, scale),
        out_shape=(
            shape((rows, cols), f32),
            shape((rows, cols), f32),
            shape((segs * modes, cols), f32),
            shape((segs * modes, cols), f32),
            shape((2, modes, cols), f32),
            shape((2, modes, cols), f32),
            shape((2, modes, cols), f32),
        ),
        in_specs=[whole] * 6,
        out_specs=(whole,) * 7,
        scratch_shapes=[
            tile,
            tile,
            pltpu.VMEM((modes, LANES), f32),
            pltpu.VMEM((SEG, LANES), f32),
            pltpu.VMEM((SEG * modes, LANES), f32),
            tile,
            tile,
            pltpu.VMEM((4, modes * segs, LANES), f32),
            pltpu.VMEM((groups * SEG * SUB, LANES), f32),
        ],
        compiler_params=params,
        name="local",
    )(signal_in, gate_in, outer_gate, cotangent, residues, log_rates)
    edges = lax.all_gather(edge, "seq", axis=0)
    out_sig, out_gate, out_outer, totals = pl.pallas_call(
        functools.partial(finish_phase, scale, parts, rows),
        out_shape=(
            shape((rows, cols), jnp.bfloat16),
            shape((rows, cols), jnp.bfloat16),
            shape((rows, cols), jnp.bfloat16),
            shape((2, modes, filters), f32),
        ),
        in_specs=[whole] * 13,
        out_specs=(whole,) * 4,
        scratch_shapes=[
            pltpu.VMEM((2, modes, cols), f32),
            pltpu.VMEM((modes, LANES), f32),
            tile,
            tile,
            pltpu.VMEM((segs * modes, LANES), f32),
            pltpu.VMEM((segs * modes, LANES), f32),
        ],
        compiler_params=params,
        name="finish",
    )(signal_in, gate_in, cotangent, residues, log_rates, conv, grad, xs, ys, edges, edge, moment, gsum)
    totals = norm * lax.psum(totals, ("seq", "chan"))
    return out_sig, out_gate, out_outer, totals[0], totals[1]


def solution(mesh):
    placed = (P("seq", "chan"), P("seq", "chan"), P("seq", "chan"), P("seq", "chan"), P(), P())
    return jax.shard_map(
        on_device,
        mesh=mesh,
        in_specs=placed,
        out_specs=(P("seq", "chan"), P("seq", "chan"), P("seq", "chan"), P(), P()),
        check_vma=False,
    )
```

```python
import functools
import math

import jax
import jax.numpy as jnp
from jax import lax
from jax.experimental import pallas as pl
from jax.experimental.pallas import tpu as pltpu
from jax.sharding import PartitionSpec as P

LANES = 128
SUB = 8
SEG = 16
f32 = jnp.float32
MESH = pl.DeviceIdType.MESH


def rows_of(ref, first, stride):
    return ref[pl.ds(first, SUB, stride=stride), :]


def spread(ref, row):
    return jnp.broadcast_to(ref[pl.ds(row, 1), :], (SUB, LANES))


def filter_lanes(block, cols, filters):
    start = lax.axis_index("chan") * cols + block * LANES
    return pl.ds(pl.multiple_of(lax.rem(start, filters), LANES), LANES)


def block_lanes(block):
    return pl.ds(pl.multiple_of(block * LANES, LANES), LANES)


def tree(values):
    while len(values) > 1:
        values = [values[i] + values[i + 1] for i in range(0, len(values), 2)]
    return values[0]


def state_block(scale, block, fl, sig, gate, outer, cot, res, logr, g_s, w_s, a_s, h_s, pw_s, st, lag_s, xs, ys, edge,
                moment, gsum):
    rows = sig.shape[0]
    modes = res.shape[0]
    segs = rows // SEG
    groups = segs // SUB
    g_s[...] = (sig[...].astype(f32) * gate[...].astype(f32)).astype(jnp.bfloat16).astype(f32)
    w_s[...] = (cot[...].astype(f32) * outer[...].astype(f32)).astype(jnp.bfloat16).astype(f32)
    rate = jnp.exp(logr[:, fl])
    amp = res[:, fl] * scale
    a = jnp.exp(-rate)
    a_s[...] = a
    power = jnp.ones((modes, LANES), f32)
    for u in range(SEG):
        pw_s[u * modes : (u + 1) * modes, :] = power
        h_s[u : u + 1, :] = jnp.sum(amp * power, 0, keepdims=True)
        power = power * a
    seg_decay = power

    @pl.loop(0, groups)
    def _(group):
        base = group * (SUB * SEG)
        for half in range(0, modes, SUB):
            decay = [spread(a_s, half + k) for k in range(SUB)]
            zero = jnp.zeros((SUB, LANES), f32)
            x, z, y, v = ([zero] * SUB for _ in range(4))
            for j in range(SEG):
                gj = rows_of(g_s, base + j, SEG)
                wj = rows_of(w_s, base + SEG - 1 - j, SEG)
                for k in range(SUB):
                    x[k] = decay[k] * (x[k] + gj)
                    z[k] = decay[k] * z[k] + x[k]
                    t = decay[k] * y[k]
                    y[k] = t + wj
                    v[k] = decay[k] * v[k] + t
            for k in range(SUB):
                at = pl.ds(pl.multiple_of((half + k) * segs + group * SUB, SUB), SUB)
                st[0, at, :] = x[k]
                st[1, at, :] = z[k]
                st[2, at, :] = y[k]
                st[3, at, :] = v[k]
        g = [rows_of(g_s, base + j, SEG) for j in range(SEG)]
        w = [rows_of(w_s, base + j, SEG) for j in range(SEG)]
        for u in range(SEG):
            total = w[u] * g[0]
            for j in range(u + 1, SEG):
                total = total + w[j] * g[j - u]
            lag_s[pl.ds(pl.multiple_of((group * SEG + u) * SUB, SUB), SUB), :] = total

    gr = jnp.zeros((modes, LANES), f32)
    gl = jnp.zeros((modes, LANES), f32)
    for u in range(SEG):
        total = lag_s[u * SUB : (u + 1) * SUB, :]
        for group in range(1, groups):
            first = (group * SEG + u) * SUB
            total = total + lag_s[first : first + SUB, :]
        term = jnp.sum(total, 0, keepdims=True) * pw_s[u * modes : (u + 1) * modes, :]
        gr = gr + term
        if u > 0:
            gl = gl + float(u) * term
    x = jnp.zeros((modes, LANES), f32)
    xd = x
    for seg in range(segs):
        at = pl.ds(seg, modes, stride=segs)
        e, d, y, v = (st[i, at, :] for i in range(4))
        xs[seg * modes : (seg + 1) * modes, :] = x
        if seg > 0:
            gr = gr + x * y
            gl = gl + (xd * y + x * v)
        xd = seg_decay * (xd + float(SEG) * x) + d
        x = seg_decay * x + e
    y = jnp.zeros((modes, LANES), f32)
    yv = y
    for seg in reversed(range(segs)):
        at = pl.ds(seg, modes, stride=segs)
        ys[seg * modes : (seg + 1) * modes, :] = y
        yv = st[3, at, :] + seg_decay * (yv + float(SEG) * y)
        y = st[2, at, :] + seg_decay * y
    edge[0, block] = x
    edge[1, block] = y
    moment[0] = xd
    moment[1] = yv
    gsum[0] = gr
    gsum[1] = gl


def inner_block(rows, g_s, w_s, h_s, conv, grad):
    @pl.loop(0, rows // (SEG * SUB))
    def _(group):
        base = group * (SUB * SEG)
        h = [spread(h_s, u) for u in range(SEG)]
        g = [rows_of(g_s, base + j, SEG) for j in range(SEG)]
        for j in range(SEG):
            forward = h[0] * g[j]
            for u in range(1, j + 1):
                forward = forward + h[u] * g[j - u]
            conv[pl.ds(base + j, SUB, stride=SEG), :] = forward
        w = [rows_of(w_s, base + j, SEG) for j in range(SEG)]
        for j in range(SEG):
            backward = h[0] * w[j]
            for u in range(1, SEG - j):
                backward = backward + h[u] * w[j + u]
            grad[pl.ds(base + j, SUB, stride=SEG), :] = backward


def gradient_block(scale, parts, span, block, fl, edges, edge, moment, gsum, res, logr, totals, carry):
    place = lax.axis_index("seq")
    rate = jnp.exp(logr[:, fl])
    x0 = jnp.zeros(rate.shape, f32)
    xm = x0
    y0 = x0
    for other in range(parts):
        ahead = jnp.maximum(place - 1 - other, 0).astype(f32) * float(span)
        behind = jnp.maximum(other - place - 1, 0).astype(f32) * float(span)
        value = edges[other, block]
        e = jnp.where(other < place, value, 0.0) * jnp.exp(-rate * ahead)
        x0 = x0 + e
        xm = xm + ahead * e
        y0 = y0 + jnp.where(other > place, value, 0.0) * jnp.exp(-rate * behind)
    carry[0] = x0
    carry[1] = y0
    w = edge[1, block]
    gr = gsum[0] + x0 * w
    gl = gsum[1] + x0 * moment[1] + xm * w + moment[0] * y0
    totals[0, :, fl] = totals[0, :, fl] + scale * gr
    totals[1, :, fl] = totals[1, :, fl] - scale * (res[:, fl] * rate) * gl


def output_block(scale, fl, sig, gate, cot, res, logr, conv, grad, xs, ys, carry, out_sig, out_gate, out_outer,
                 a_s, p_s, q_s):
    rows = sig.shape[0]
    modes = res.shape[0]
    segs = rows // SEG
    rate = jnp.exp(logr[:, fl])
    amp = res[:, fl] * scale
    a_s[...] = jnp.exp(-rate)
    seg_decay = jnp.exp(-rate * float(SEG))
    p = amp * carry[0]
    q = amp * carry[1]
    for seg in range(segs):
        at = slice(seg * modes, (seg + 1) * modes)
        p_s[at, :] = amp * xs[at, :] + p
        p = p * seg_decay
        back = segs - 1 - seg
        at = slice(back * modes, (back + 1) * modes)
        q_s[at, :] = amp * ys[at, :] + q
        q = q * seg_decay

    @pl.loop(0, segs // SUB)
    def _(group):
        base = group * (SUB * SEG)
        for half in range(0, modes, SUB):
            decay = [spread(a_s, half + k) for k in range(SUB)]
            p = [rows_of(p_s, group * (SUB * modes) + half + k, modes) for k in range(SUB)]
            q = [rows_of(q_s, group * (SUB * modes) + half + k, modes) for k in range(SUB)]
            for j in range(SEG):
                at = pl.ds(base + j, SUB, stride=SEG)
                conv[at, :] = conv[at, :] + tree(p)
                q = [decay[k] * q[k] for k in range(SUB)]
                at = pl.ds(base + SEG - 1 - j, SUB, stride=SEG)
                grad[at, :] = grad[at, :] + tree(q)
                if j < SEG - 1:
                    p = [decay[k] * p[k] for k in range(SUB)]

    d = grad[...]
    out_sig[...] = (d * gate[...].astype(f32)).astype(jnp.bfloat16)
    out_gate[...] = (d * sig[...].astype(f32)).astype(jnp.bfloat16)
    out_outer[...] = (conv[...] * cot[...].astype(f32)).astype(jnp.bfloat16)


def whole_kernel(
    scale, norm, parts, groups_chan,
    sig_h, gate_h, outer_h, cot_h, res_h, logr_h,
    out_sig_h, out_gate_h, out_outer_h, out_res, out_rate,
    ins, params, outs, g_s, w_s, conv, grad, xs, ys, edge, edges, moment, gsum, carry, h_s,
    a_s, pw_s, st, lag_s, p_s, q_s, totals, pieces, landed, slots, final,
    in_sem, param_sem, out_sem, edge_send, edge_recv, rs_send, rs_recv, mid_send, mid_recv, end_send, end_recv,
):
    rows, cols = sig_h.shape
    modes, filters = res_h.shape
    blocks = cols // LANES
    place = lax.axis_index("seq")
    column = lax.axis_index("chan")
    barrier = pltpu.get_barrier_semaphore()

    def along(axis, index, size, d):
        return {axis: lax.rem(index + d, size)}

    def remote(src, dst, send, recv, device):
        return pltpu.make_async_remote_copy(
            src_ref=src, dst_ref=dst, send_sem=send, recv_sem=recv, device_id=device, device_id_type=MESH
        )

    for d in range(1, parts):
        pl.semaphore_signal(barrier, inc=1, device_id=along("seq", place, parts, d), device_id_type=MESH)
    for d in range(1, groups_chan):
        pl.semaphore_signal(barrier, inc=1, device_id=along("chan", column, groups_chan, d), device_id_type=MESH)

    param_copies = [
        pltpu.make_async_copy(ref, params.at[i], param_sem.at[i]) for i, ref in enumerate((res_h, logr_h))
    ]
    for copy in param_copies:
        copy.start()

    def fetch(i, ref, block):
        return pltpu.make_async_copy(ref.at[:, block_lanes(block)], ins.at[i, block], in_sem.at[i, block])

    whole_inputs = (sig_h, gate_h, outer_h, cot_h)

    @pl.loop(0, blocks)
    def _(block):
        for i, ref in enumerate(whole_inputs):
            fetch(i, ref, block).start()

    for copy in param_copies:
        copy.wait()
    pl.semaphore_wait(barrier, parts - 1 + groups_chan - 1)
    res, logr = params.at[0], params.at[1]

    def edge_copy(d, block):
        other = lax.rem(place + d, parts)
        which = jnp.where(other > place, 0, 1)
        if block is None:
            src, dst = edge.at[which], edges.at[place]
        else:
            src, dst = edge.at[which, block], edges.at[place, block]
        return remote(src, dst, edge_send.at[d], edge_recv.at[d], {"seq": other})

    @pl.loop(0, blocks)
    def _(block):
        for i, ref in enumerate(whole_inputs):
            fetch(i, ref, block).wait()
        sig, gate, outer, cot = (ins.at[i, block] for i in range(4))
        state_block(
            scale, block, filter_lanes(block, cols, filters), sig, gate, outer, cot, res, logr,
            g_s.at[block], w_s.at[block], a_s, h_s.at[block], pw_s, st, lag_s, xs.at[block], ys.at[block], edge,
            moment.at[block], gsum.at[block],
        )
        for d in range(1, parts):
            edge_copy(d, block).start()

    def inner(first, last):
        @pl.loop(first, last)
        def _(block):
            inner_block(rows, g_s.at[block], w_s.at[block], h_s.at[block], conv.at[block], grad.at[block])

    early = (blocks + 1) // 2
    inner(0, early)
    for d in range(1, parts):
        source = lax.rem(place + parts - d, parts)
        remote(edge.at[0], edges.at[source], edge_send.at[d], edge_recv.at[d], {"seq": source}).wait_recv()
    totals[...] = jnp.zeros_like(totals)
    edges[place] = jnp.zeros_like(edge[0])

    @pl.loop(0, blocks)
    def _(block):
        gradient_block(
            scale, parts, rows, block, filter_lanes(block, cols, filters), edges, edge, moment.at[block],
            gsum.at[block], res, logr, totals, carry.at[block],
        )

    size = 2 * modes // parts
    for p in range(parts):
        which, first = divmod(p * size, modes)
        pieces[p] = totals[which, first : first + size, :]

    def scatter(d):
        other = lax.rem(place + d, parts)
        return remote(pieces.at[other], landed.at[d], rs_send.at[d], rs_recv.at[d], {"seq": other})

    def middle(d):
        other = lax.rem(column + d, groups_chan)
        return remote(slots.at[column], slots.at[column], mid_send.at[d], mid_recv.at[d], {"chan": other})

    def middle_arrival(d):
        source = lax.rem(column + groups_chan - d, groups_chan)
        return remote(slots.at[source], slots.at[source], mid_send.at[d], mid_recv.at[d], {"chan": source})

    def ending(d):
        other = lax.rem(place + d, parts)
        return remote(final.at[place], final.at[place], end_send.at[d], end_recv.at[d], {"seq": other})

    def ending_arrival(d):
        source = lax.rem(place + parts - d, parts)
        return remote(final.at[source], final.at[source], end_send.at[d], end_recv.at[d], {"seq": source})

    for d in range(1, parts):
        scatter(d).start()
    inner(early, blocks)

    def put(i, ref, block):
        return pltpu.make_async_copy(outs.at[i, block], ref.at[:, block_lanes(block)], out_sem.at[i, block])

    whole_outputs = (out_sig_h, out_gate_h, out_outer_h)

    def outputs(first, last):
        if first == last:
            return

        @pl.loop(first, last)
        def _(block):
            output_block(
                scale, filter_lanes(block, cols, filters), ins.at[0, block], ins.at[1, block], ins.at[3, block],
                res, logr, conv.at[block], grad.at[block], xs.at[block], ys.at[block], carry.at[block],
                outs.at[0, block], outs.at[1, block], outs.at[2, block], a_s, p_s, q_s,
            )
            for i, ref in enumerate(whole_outputs):
                put(i, ref, block).start()

    first_stop = blocks // 8
    second_stop = blocks - blocks // 4
    outputs(0, first_stop)
    for d in range(1, parts):
        scatter(d).wait_recv()
    mine = pieces[place]
    for d in range(1, parts):
        mine = mine + landed[d]
    slots[column] = mine
    for d in range(1, groups_chan):
        middle(d).start()
    outputs(first_stop, second_stop)
    for d in range(1, groups_chan):
        middle_arrival(d).wait_recv()
    summed = slots[0]
    for other in range(1, groups_chan):
        summed = summed + slots[other]
    final[place] = norm * summed
    for d in range(1, parts):
        ending(d).start()
    outputs(second_stop, blocks)
    for d in range(1, parts):
        ending_arrival(d).wait_recv()
    for p in range(parts):
        which, first = divmod(p * size, modes)
        target = (out_res, out_rate)[which]
        target[first : first + size, :] = final[p]

    for d in range(1, parts):
        edge_copy(d, None).wait_send()
        scatter(d).wait_send()
        ending(d).wait_send()
    for d in range(1, groups_chan):
        middle(d).wait_send()

    @pl.loop(0, blocks)
    def _(block):
        for i, ref in enumerate(whole_outputs):
            put(i, ref, block).wait()


def on_device(signal_in, gate_in, outer_gate, cotangent, residues, log_rates):
    parts = lax.axis_size("seq")
    groups_chan = lax.axis_size("chan")
    rows, cols = signal_in.shape
    modes, filters = residues.shape
    total = parts * rows
    blocks = cols // LANES
    segs = rows // SEG
    groups = segs // SUB
    size = 2 * modes // parts
    scale = float(total) ** (-0.5)
    norm = float(total * cols * groups_chan // filters) ** (-0.5)
    whole = pl.BlockSpec(memory_space=pltpu.VMEM)
    far = pl.BlockSpec(memory_space=pl.ANY)
    shape = jax.ShapeDtypeStruct
    small = pltpu.VMEM((modes, LANES), f32)
    tiles = pltpu.VMEM((blocks, rows, LANES), f32)
    states = pltpu.VMEM((blocks, segs * modes, LANES), f32)
    pair = pltpu.VMEM((blocks, 2, modes, LANES), f32)
    dma = pltpu.SemaphoreType.DMA
    return pl.pallas_call(
        functools.partial(whole_kernel, scale, norm, parts, groups_chan),
        out_shape=(
            shape((rows, cols), jnp.bfloat16),
            shape((rows, cols), jnp.bfloat16),
            shape((rows, cols), jnp.bfloat16),
            shape((modes, filters), f32),
            shape((modes, filters), f32),
        ),
        in_specs=[pl.BlockSpec(memory_space=pltpu.HBM)] * 6,
        out_specs=(far, far, far, whole, whole),
        scratch_shapes=[
            pltpu.VMEM((4, blocks, rows, LANES), jnp.bfloat16),
            pltpu.VMEM((2, modes, filters), f32),
            pltpu.VMEM((3, blocks, rows, LANES), jnp.bfloat16),
            tiles,
            tiles,
            tiles,
            tiles,
            states,
            states,
            pltpu.VMEM((2, blocks, modes, LANES), f32),
            pltpu.VMEM((parts, blocks, modes, LANES), f32),
            pair,
            pair,
            pair,
            pltpu.VMEM((blocks, SEG, LANES), f32),
            small,
            pltpu.VMEM((SEG * modes, LANES), f32),
            pltpu.VMEM((4, modes * segs, LANES), f32),
            pltpu.VMEM((groups * SEG * SUB, LANES), f32),
            pltpu.VMEM((segs * modes, LANES), f32),
            pltpu.VMEM((segs * modes, LANES), f32),
            pltpu.VMEM((2, modes, filters), f32),
            pltpu.VMEM((parts, size, filters), f32),
            pltpu.VMEM((parts, size, filters), f32),
            pltpu.VMEM((groups_chan, size, filters), f32),
            pltpu.VMEM((parts, size, filters), f32),
            dma((4, blocks)),
            dma((2,)),
            dma((3, blocks)),
            dma((parts,)),
            dma((parts,)),
            dma((parts,)),
            dma((parts,)),
            dma((groups_chan,)),
            dma((groups_chan,)),
            dma((parts,)),
            dma((parts,)),
        ],
        compiler_params=pltpu.CompilerParams(
            vmem_limit_bytes=48 * 1024 * 1024, collective_id=0, has_side_effects=True
        ),
        name="whole",
    )(signal_in, gate_in, outer_gate, cotangent, residues, log_rates)


def solution(mesh):
    placed = (P("seq", "chan"), P("seq", "chan"), P("seq", "chan"), P("seq", "chan"), P(), P())
    return jax.shard_map(
        on_device,
        mesh=mesh,
        in_specs=placed,
        out_specs=(P("seq", "chan"), P("seq", "chan"), P("seq", "chan"), P(), P()),
        check_vma=False,
    )
```

```python
import functools
import math

import jax
import jax.numpy as jnp
from jax import lax
from jax.experimental import pallas as pl
from jax.experimental.pallas import tpu as pltpu
from jax.sharding import PartitionSpec as P

LANES = 128
SUB = 8
SEG = 16
f32 = jnp.float32
MESH = pl.DeviceIdType.MESH


def rows_of(ref, first, stride):
    return ref[pl.ds(first, SUB, stride=stride), :]


def spread(ref, row):
    return jnp.broadcast_to(ref[pl.ds(row, 1), :], (SUB, LANES))


def filter_lanes(block, cols, filters):
    start = lax.axis_index("chan") * cols + block * LANES
    return pl.ds(pl.multiple_of(lax.rem(start, filters), LANES), LANES)


def block_lanes(block):
    return pl.ds(pl.multiple_of(block * LANES, LANES), LANES)


def tree(values):
    while len(values) > 1:
        values = [values[i] + values[i + 1] for i in range(0, len(values), 2)]
    return values[0]


def state_block(scale, block, fl, sig, gate, outer, cot, res, logr, g_s, w_s, a_s, h_s, pw_s, st, lag_s, xs, ys, edge,
                moment, gsum):
    rows = sig.shape[0]
    modes = res.shape[0]
    segs = rows // SEG
    groups = segs // SUB
    g_s[...] = (sig[...].astype(f32) * gate[...].astype(f32)).astype(jnp.bfloat16).astype(f32)
    w_s[...] = (cot[...].astype(f32) * outer[...].astype(f32)).astype(jnp.bfloat16).astype(f32)
    rate = jnp.exp(logr[:, fl])
    amp = res[:, fl] * scale
    a = jnp.exp(-rate)
    a_s[...] = a
    power = jnp.ones((modes, LANES), f32)
    for u in range(SEG):
        pw_s[u * modes : (u + 1) * modes, :] = power
        h_s[u : u + 1, :] = jnp.sum(amp * power, 0, keepdims=True)
        power = power * a
    seg_decay = power

    @pl.loop(0, groups)
    def _(group):
        base = group * (SUB * SEG)
        for half in range(0, modes, SUB):
            decay = [spread(a_s, half + k) for k in range(SUB)]
            zero = jnp.zeros((SUB, LANES), f32)
            x, z, y, v = ([zero] * SUB for _ in range(4))
            for j in range(SEG):
                gj = rows_of(g_s, base + j, SEG)
                wj = rows_of(w_s, base + SEG - 1 - j, SEG)
                for k in range(SUB):
                    x[k] = decay[k] * (x[k] + gj)
                    z[k] = decay[k] * z[k] + x[k]
                    t = decay[k] * y[k]
                    y[k] = t + wj
                    v[k] = decay[k] * v[k] + t
            for k in range(SUB):
                at = pl.ds(pl.multiple_of((half + k) * segs + group * SUB, SUB), SUB)
                st[0, at, :] = x[k]
                st[1, at, :] = z[k]
                st[2, at, :] = y[k]
                st[3, at, :] = v[k]
        g = [rows_of(g_s, base + j, SEG) for j in range(SEG)]
        w = [rows_of(w_s, base + j, SEG) for j in range(SEG)]
        for u in range(SEG):
            total = w[u] * g[0]
            for j in range(u + 1, SEG):
                total = total + w[j] * g[j - u]
            lag_s[pl.ds(pl.multiple_of((group * SEG + u) * SUB, SUB), SUB), :] = total

    gr = jnp.zeros((modes, LANES), f32)
    gl = jnp.zeros((modes, LANES), f32)
    for u in range(SEG):
        total = lag_s[u * SUB : (u + 1) * SUB, :]
        for group in range(1, groups):
            first = (group * SEG + u) * SUB
            total = total + lag_s[first : first + SUB, :]
        term = jnp.sum(total, 0, keepdims=True) * pw_s[u * modes : (u + 1) * modes, :]
        gr = gr + term
        if u > 0:
            gl = gl + float(u) * term
    x = jnp.zeros((modes, LANES), f32)
    xd = x
    for seg in range(segs):
        at = pl.ds(seg, modes, stride=segs)
        e, d, y, v = (st[i, at, :] for i in range(4))
        xs[seg * modes : (seg + 1) * modes, :] = x
        if seg > 0:
            gr = gr + x * y
            gl = gl + (xd * y + x * v)
        xd = seg_decay * (xd + float(SEG) * x) + d
        x = seg_decay * x + e
    y = jnp.zeros((modes, LANES), f32)
    yv = y
    for seg in reversed(range(segs)):
        at = pl.ds(seg, modes, stride=segs)
        ys[seg * modes : (seg + 1) * modes, :] = y
        yv = st[3, at, :] + seg_decay * (yv + float(SEG) * y)
        y = st[2, at, :] + seg_decay * y
    edge[0, block] = x
    edge[1, block] = y
    moment[0] = xd
    moment[1] = yv
    gsum[0] = gr
    gsum[1] = gl


def inner_block(rows, g_s, w_s, h_s, conv, grad):
    @pl.loop(0, rows // (SEG * SUB))
    def _(group):
        base = group * (SUB * SEG)
        h = [spread(h_s, u) for u in range(SEG)]
        g = [rows_of(g_s, base + j, SEG) for j in range(SEG)]
        for j in range(SEG):
            forward = h[0] * g[j]
            for u in range(1, j + 1):
                forward = forward + h[u] * g[j - u]
            conv[pl.ds(base + j, SUB, stride=SEG), :] = forward
        w = [rows_of(w_s, base + j, SEG) for j in range(SEG)]
        for j in range(SEG):
            backward = h[0] * w[j]
            for u in range(1, SEG - j):
                backward = backward + h[u] * w[j + u]
            grad[pl.ds(base + j, SUB, stride=SEG), :] = backward


def gradient_block(scale, parts, span, block, fl, edges, edge, moment, gsum, res, logr, totals, carry):
    place = lax.axis_index("seq")
    rate = jnp.exp(logr[:, fl])
    x0 = jnp.zeros(rate.shape, f32)
    xm = x0
    y0 = x0
    for other in range(parts):
        ahead = jnp.maximum(place - 1 - other, 0).astype(f32) * float(span)
        behind = jnp.maximum(other - place - 1, 0).astype(f32) * float(span)
        value = edges[other, block]
        e = jnp.where(other < place, value, 0.0) * jnp.exp(-rate * ahead)
        x0 = x0 + e
        xm = xm + ahead * e
        y0 = y0 + jnp.where(other > place, value, 0.0) * jnp.exp(-rate * behind)
    carry[0] = x0
    carry[1] = y0
    w = edge[1, block]
    gr = gsum[0] + x0 * w
    gl = gsum[1] + x0 * moment[1] + xm * w + moment[0] * y0
    totals[0, :, fl] = totals[0, :, fl] + scale * gr
    totals[1, :, fl] = totals[1, :, fl] - scale * (res[:, fl] * rate) * gl


def output_block(scale, fl, res, logr, conv, grad, xs, ys, carry, a_s, p_s, q_s):
    rows = conv.shape[0]
    modes = res.shape[0]
    segs = rows // SEG
    rate = jnp.exp(logr[:, fl])
    amp = res[:, fl] * scale
    a_s[...] = jnp.exp(-rate)
    seg_decay = jnp.exp(-rate * float(SEG))
    p = amp * carry[0]
    q = amp * carry[1]
    for seg in range(segs):
        at = slice(seg * modes, (seg + 1) * modes)
        p_s[at, :] = amp * xs[at, :] + p
        p = p * seg_decay
        back = segs - 1 - seg
        at = slice(back * modes, (back + 1) * modes)
        q_s[at, :] = amp * ys[at, :] + q
        q = q * seg_decay

    @pl.loop(0, segs // SUB)
    def _(group):
        base = group * (SUB * SEG)
        for half in range(0, modes, SUB):
            decay = [spread(a_s, half + k) for k in range(SUB)]
            p = [rows_of(p_s, group * (SUB * modes) + half + k, modes) for k in range(SUB)]
            q = [rows_of(q_s, group * (SUB * modes) + half + k, modes) for k in range(SUB)]
            for j in range(SEG):
                at = pl.ds(base + j, SUB, stride=SEG)
                conv[at, :] = conv[at, :] + tree(p)
                q = [decay[k] * q[k] for k in range(SUB)]
                at = pl.ds(base + SEG - 1 - j, SUB, stride=SEG)
                grad[at, :] = grad[at, :] + tree(q)
                if j < SEG - 1:
                    p = [decay[k] * p[k] for k in range(SUB)]


def whole_kernel(
    scale, norm, parts, groups_chan,
    sig_h, gate_h, outer_h, cot_h, res_h, logr_h,
    conv_h, grad_h, sums_h,
    ins, params, g_s, w_s, conv, grad, xs, ys, edge, edges, moment, gsum, carry, h_s,
    a_s, pw_s, st, lag_s, p_s, q_s, totals, pieces, landed, slots, final,
    in_sem, param_sem, out_sem, edge_send, edge_recv, rs_send, rs_recv, mid_send, mid_recv, end_send, end_recv,
):
    rows, cols = sig_h.shape
    modes, filters = res_h.shape
    blocks = cols // LANES
    place = lax.axis_index("seq")
    column = lax.axis_index("chan")
    pairs = pair_size(groups_chan)
    barrier = pltpu.get_barrier_semaphore()

    def remote(src, dst, send, recv, device):
        return pltpu.make_async_remote_copy(
            src_ref=src, dst_ref=dst, send_sem=send, recv_sem=recv, device_id=device, device_id_type=MESH
        )

    low = lax.rem(column, pairs)
    high = column // pairs
    upper = groups_chan // pairs
    team = parts * pairs
    member = place * pairs + low

    def mate(index):
        return {"seq": index // pairs, "chan": high * pairs + lax.rem(index, pairs)}

    def tower(index):
        return {"chan": index * pairs + low}

    for d in range(1, team):
        pl.semaphore_signal(barrier, inc=1, device_id=mate(lax.rem(member + d, team)), device_id_type=MESH)
    for d in range(1, upper):
        pl.semaphore_signal(barrier, inc=1, device_id=tower(lax.rem(high + d, upper)), device_id_type=MESH)

    param_copies = [
        pltpu.make_async_copy(ref, params.at[i], param_sem.at[i]) for i, ref in enumerate((res_h, logr_h))
    ]
    for copy in param_copies:
        copy.start()

    def fetch(i, ref, block):
        return pltpu.make_async_copy(ref.at[:, block_lanes(block)], ins.at[i, block], in_sem.at[i, block])

    whole_inputs = (sig_h, gate_h, outer_h, cot_h)

    @pl.loop(0, blocks)
    def _(block):
        for i, ref in enumerate(whole_inputs):
            fetch(i, ref, block).start()

    for copy in param_copies:
        copy.wait()
    pl.semaphore_wait(barrier, team - 1 + upper - 1)
    res, logr = params.at[0], params.at[1]

    def edge_copy(d, block):
        other = lax.rem(place + d, parts)
        which = jnp.where(other > place, 0, 1)
        if block is None:
            src, dst = edge.at[which], edges.at[place]
        else:
            src, dst = edge.at[which, block], edges.at[place, block]
        return remote(src, dst, edge_send.at[d], edge_recv.at[d], {"seq": other})

    @pl.loop(0, blocks)
    def _(block):
        for i, ref in enumerate(whole_inputs):
            fetch(i, ref, block).wait()
        sig, gate, outer, cot = (ins.at[i, block] for i in range(4))
        state_block(
            scale, block, filter_lanes(block, cols, filters), sig, gate, outer, cot, res, logr,
            g_s.at[block], w_s.at[block], a_s, h_s.at[block], pw_s, st, lag_s, xs.at[block], ys.at[block], edge,
            moment.at[block], gsum.at[block],
        )
        for d in range(1, parts):
            edge_copy(d, block).start()

    def inner(first, last):
        @pl.loop(first, last)
        def _(block):
            inner_block(rows, g_s.at[block], w_s.at[block], h_s.at[block], conv.at[block], grad.at[block])

    early = (blocks + 1) // 2
    inner(0, early)
    for d in range(1, parts):
        source = lax.rem(place + parts - d, parts)
        remote(edge.at[0], edges.at[source], edge_send.at[d], edge_recv.at[d], {"seq": source}).wait_recv()
    totals[...] = jnp.zeros_like(totals)
    edges[place] = jnp.zeros_like(edge[0])

    @pl.loop(0, blocks)
    def _(block):
        gradient_block(
            scale, parts, rows, block, filter_lanes(block, cols, filters), edges, edge, moment.at[block],
            gsum.at[block], res, logr, totals, carry.at[block],
        )

    size = 2 * modes // team
    for p in range(team):
        which, first = divmod(p * size, modes)
        pieces[p] = totals[which, first : first + size, :]

    def scatter(d):
        other = lax.rem(member + d, team)
        return remote(pieces.at[other], landed.at[d], rs_send.at[d], rs_recv.at[d], mate(other))

    def middle(d, back=False):
        other = lax.rem(high + (upper - d if back else d), upper)
        slot = slots.at[other if back else high]
        return remote(slot, slot, mid_send.at[d], mid_recv.at[d], tower(other))

    def ending(d, back=False):
        other = lax.rem(member + (team - d if back else d), team)
        slot = final.at[other if back else member]
        return remote(slot, slot, end_send.at[d], end_recv.at[d], mate(other))

    for d in range(1, team):
        scatter(d).start()
    inner(early, blocks)

    def put(i, block):
        src, dst = ((conv, conv_h), (grad, grad_h))[i]
        return pltpu.make_async_copy(src.at[block], dst.at[:, block_lanes(block)], out_sem.at[i, block])

    def outputs(first, last):
        if first == last:
            return

        @pl.loop(first, last)
        def _(block):
            output_block(
                scale, filter_lanes(block, cols, filters), res, logr, conv.at[block], grad.at[block], xs.at[block],
                ys.at[block], carry.at[block], a_s, p_s, q_s,
            )
            for i in range(2):
                put(i, block).start()

    first_stop = blocks // 8
    second_stop = blocks - blocks // 4
    outputs(0, first_stop)
    for d in range(1, team):
        scatter(d).wait_recv()
    mine = pieces[member]
    for d in range(1, team):
        mine = mine + landed[d]
    slots[high] = mine
    for d in range(1, upper):
        middle(d).start()
    outputs(first_stop, second_stop)
    for d in range(1, upper):
        middle(d, back=True).wait_recv()
    summed = slots[0]
    for other in range(1, upper):
        summed = summed + slots[other]
    final[member] = norm * summed
    for d in range(1, team):
        ending(d).start()
    outputs(second_stop, blocks)
    for d in range(1, team):
        ending(d, back=True).wait_recv()
    for p in range(team):
        which, first = divmod(p * size, modes)
        sums_h[which, first : first + size, :] = final[p]

    for d in range(1, parts):
        edge_copy(d, None).wait_send()
    for d in range(1, team):
        scatter(d).wait_send()
        ending(d).wait_send()
    for d in range(1, upper):
        middle(d).wait_send()

    @pl.loop(0, blocks)
    def _(block):
        for i in range(2):
            put(i, block).wait()


def gate_kernel(conv, grad, sig, gate, cot, sums, out_sig, out_gate, out_outer, out_res, out_rate):
    d = grad[...]
    out_sig[...] = (d * gate[...].astype(f32)).astype(jnp.bfloat16)
    out_gate[...] = (d * sig[...].astype(f32)).astype(jnp.bfloat16)
    out_outer[...] = (conv[...] * cot[...].astype(f32)).astype(jnp.bfloat16)
    out_res[...] = sums[0]
    out_rate[...] = sums[1]


def pair_size(columns):
    return 2 if columns % 2 == 0 else 1


def on_device(signal_in, gate_in, outer_gate, cotangent, residues, log_rates):
    parts = lax.axis_size("seq")
    groups_chan = lax.axis_size("chan")
    rows, cols = signal_in.shape
    modes, filters = residues.shape
    total = parts * rows
    blocks = cols // LANES
    segs = rows // SEG
    groups = segs // SUB
    pairs = pair_size(groups_chan)
    team = parts * pairs
    upper = groups_chan // pairs
    size = 2 * modes // team
    scale = float(total) ** (-0.5)
    norm = float(total * cols * groups_chan // filters) ** (-0.5)
    whole = pl.BlockSpec(memory_space=pltpu.VMEM)
    far = pl.BlockSpec(memory_space=pl.ANY)
    shape = jax.ShapeDtypeStruct
    small = pltpu.VMEM((modes, LANES), f32)
    tiles = pltpu.VMEM((blocks, rows, LANES), f32)
    states = pltpu.VMEM((blocks, segs * modes, LANES), f32)
    pair = pltpu.VMEM((blocks, 2, modes, LANES), f32)
    dma = pltpu.SemaphoreType.DMA
    conv, grad, sums = pl.pallas_call(
        functools.partial(whole_kernel, scale, norm, parts, groups_chan),
        out_shape=(
            shape((rows, cols), f32),
            shape((rows, cols), f32),
            shape((2, modes, filters), f32),
        ),
        in_specs=[pl.BlockSpec(memory_space=pltpu.HBM)] * 6,
        out_specs=(far, far, whole),
        scratch_shapes=[
            pltpu.VMEM((4, blocks, rows, LANES), jnp.bfloat16),
            pltpu.VMEM((2, modes, filters), f32),
            tiles,
            tiles,
            tiles,
            tiles,
            states,
            states,
            pltpu.VMEM((2, blocks, modes, LANES), f32),
            pltpu.VMEM((parts, blocks, modes, LANES), f32),
            pair,
            pair,
            pair,
            pltpu.VMEM((blocks, SEG, LANES), f32),
            small,
            pltpu.VMEM((SEG * modes, LANES), f32),
            pltpu.VMEM((4, modes * segs, LANES), f32),
            pltpu.VMEM((groups * SEG * SUB, LANES), f32),
            pltpu.VMEM((segs * modes, LANES), f32),
            pltpu.VMEM((segs * modes, LANES), f32),
            pltpu.VMEM((2, modes, filters), f32),
            pltpu.VMEM((team, size, filters), f32),
            pltpu.VMEM((team, size, filters), f32),
            pltpu.VMEM((upper, size, filters), f32),
            pltpu.VMEM((team, size, filters), f32),
            dma((4, blocks)),
            dma((2,)),
            dma((2, blocks)),
            dma((parts,)),
            dma((parts,)),
            dma((team,)),
            dma((team,)),
            dma((upper,)),
            dma((upper,)),
            dma((team,)),
            dma((team,)),
        ],
        compiler_params=pltpu.CompilerParams(
            collective_id=0, has_side_effects=True
        ),
        name="whole",
    )(signal_in, gate_in, outer_gate, cotangent, residues, log_rates)
    steps = 4 if blocks % 4 == 0 else 1
    tile = pl.BlockSpec((rows, cols // steps), lambda i: (0, i))
    both = pl.BlockSpec((2, modes, filters), lambda i: (0, 0, 0))
    one = pl.BlockSpec((modes, filters), lambda i: (0, 0))
    narrow = shape((rows, cols), jnp.bfloat16)
    return pl.pallas_call(
        gate_kernel,
        out_shape=(narrow, narrow, narrow, shape((modes, filters), f32), shape((modes, filters), f32)),
        grid=(steps,),
        in_specs=[tile] * 5 + [both],
        out_specs=(tile, tile, tile, one, one),
        name="gates",
    )(conv, grad, signal_in, gate_in, cotangent, sums)


def solution(mesh):
    placed = (P("seq", "chan"), P("seq", "chan"), P("seq", "chan"), P("seq", "chan"), P(), P())
    return jax.shard_map(
        on_device,
        mesh=mesh,
        in_specs=placed,
        out_specs=(P("seq", "chan"), P("seq", "chan"), P("seq", "chan"), P(), P()),
        check_vma=False,
    )
```

```python
import functools
import math

import jax
import jax.numpy as jnp
from jax import lax
from jax.experimental import pallas as pl
from jax.experimental.pallas import tpu as pltpu
from jax.sharding import PartitionSpec as P

LANES = 128
SUB = 8
SEG = 16
f32 = jnp.float32
MESH = pl.DeviceIdType.MESH


def rows_of(ref, first, stride):
    return ref[pl.ds(first, SUB, stride=stride), :]


def spread(ref, row):
    return jnp.broadcast_to(ref[pl.ds(row, 1), :], (SUB, LANES))


def filter_lanes(block, cols, filters):
    start = lax.axis_index("chan") * cols + block * LANES
    return pl.ds(pl.multiple_of(lax.rem(start, filters), LANES), LANES)


def block_lanes(block):
    return pl.ds(pl.multiple_of(block * LANES, LANES), LANES)


def tree(values):
    while len(values) > 1:
        values = [values[i] + values[i + 1] for i in range(0, len(values), 2)]
    return values[0]


def state_block(scale, block, fl, sig, gate, outer, cot, res, logr, g_s, w_s, a_s, h_s, pw_s, st, lag_s, xs, ys, edge,
                moment, gsum):
    rows = sig.shape[0]
    modes = res.shape[0]
    segs = rows // SEG
    groups = segs // SUB
    g_s[...] = (sig[...].astype(f32) * gate[...].astype(f32)).astype(jnp.bfloat16).astype(f32)
    w_s[...] = (cot[...].astype(f32) * outer[...].astype(f32)).astype(jnp.bfloat16).astype(f32)
    rate = jnp.exp(logr[:, fl])
    amp = res[:, fl] * scale
    a = jnp.exp(-rate)
    a_s[...] = a
    power = jnp.ones((modes, LANES), f32)
    for u in range(SEG):
        pw_s[u * modes : (u + 1) * modes, :] = power
        h_s[u : u + 1, :] = jnp.sum(amp * power, 0, keepdims=True)
        power = power * a
    seg_decay = power

    @pl.loop(0, groups)
    def _(group):
        base = group * (SUB * SEG)
        for half in range(0, modes, SUB):
            decay = [spread(a_s, half + k) for k in range(SUB)]
            zero = jnp.zeros((SUB, LANES), f32)
            x, z, y, v = ([zero] * SUB for _ in range(4))
            for j in range(SEG):
                gj = rows_of(g_s, base + j, SEG)
                wj = rows_of(w_s, base + SEG - 1 - j, SEG)
                for k in range(SUB):
                    x[k] = decay[k] * (x[k] + gj)
                    z[k] = decay[k] * z[k] + x[k]
                    t = decay[k] * y[k]
                    y[k] = t + wj
                    v[k] = decay[k] * v[k] + t
            for k in range(SUB):
                at = pl.ds(pl.multiple_of((half + k) * segs + group * SUB, SUB), SUB)
                st[0, at, :] = x[k]
                st[1, at, :] = z[k]
                st[2, at, :] = y[k]
                st[3, at, :] = v[k]
        g = [rows_of(g_s, base + j, SEG) for j in range(SEG)]
        w = [rows_of(w_s, base + j, SEG) for j in range(SEG)]
        for u in range(SEG):
            total = w[u] * g[0]
            for j in range(u + 1, SEG):
                total = total + w[j] * g[j - u]
            lag_s[pl.ds(pl.multiple_of((group * SEG + u) * SUB, SUB), SUB), :] = total

    gr = jnp.zeros((modes, LANES), f32)
    gl = jnp.zeros((modes, LANES), f32)
    for u in range(SEG):
        total = lag_s[u * SUB : (u + 1) * SUB, :]
        for group in range(1, groups):
            first = (group * SEG + u) * SUB
            total = total + lag_s[first : first + SUB, :]
        term = jnp.sum(total, 0, keepdims=True) * pw_s[u * modes : (u + 1) * modes, :]
        gr = gr + term
        if u > 0:
            gl = gl + float(u) * term
    x = jnp.zeros((modes, LANES), f32)
    xd = x
    for seg in range(segs):
        at = pl.ds(seg, modes, stride=segs)
        e, d, y, v = (st[i, at, :] for i in range(4))
        xs[seg * modes : (seg + 1) * modes, :] = x
        if seg > 0:
            gr = gr + x * y
            gl = gl + (xd * y + x * v)
        xd = seg_decay * (xd + float(SEG) * x) + d
        x = seg_decay * x + e
    y = jnp.zeros((modes, LANES), f32)
    yv = y
    for seg in reversed(range(segs)):
        at = pl.ds(seg, modes, stride=segs)
        ys[seg * modes : (seg + 1) * modes, :] = y
        yv = st[3, at, :] + seg_decay * (yv + float(SEG) * y)
        y = st[2, at, :] + seg_decay * y
    edge[0, block] = x
    edge[1, block] = y
    moment[0] = xd
    moment[1] = yv
    gsum[0] = gr
    gsum[1] = gl


def inner_block(rows, g_s, w_s, h_s, conv, grad):
    @pl.loop(0, rows // (SEG * SUB))
    def _(group):
        base = group * (SUB * SEG)
        h = [spread(h_s, u) for u in range(SEG)]
        g = [rows_of(g_s, base + j, SEG) for j in range(SEG)]
        for j in range(SEG):
            forward = h[0] * g[j]
            for u in range(1, j + 1):
                forward = forward + h[u] * g[j - u]
            conv[pl.ds(base + j, SUB, stride=SEG), :] = forward
        w = [rows_of(w_s, base + j, SEG) for j in range(SEG)]
        for j in range(SEG):
            backward = h[0] * w[j]
            for u in range(1, SEG - j):
                backward = backward + h[u] * w[j + u]
            grad[pl.ds(base + j, SUB, stride=SEG), :] = backward


def gradient_block(scale, parts, span, block, fl, edges, edge, moment, gsum, res, logr, totals, carry):
    place = lax.axis_index("seq")
    rate = jnp.exp(logr[:, fl])
    x0 = jnp.zeros(rate.shape, f32)
    xm = x0
    y0 = x0
    for other in range(parts):
        ahead = jnp.maximum(place - 1 - other, 0).astype(f32) * float(span)
        behind = jnp.maximum(other - place - 1, 0).astype(f32) * float(span)
        value = edges[other, block]
        e = jnp.where(other < place, value, 0.0) * jnp.exp(-rate * ahead)
        x0 = x0 + e
        xm = xm + ahead * e
        y0 = y0 + jnp.where(other > place, value, 0.0) * jnp.exp(-rate * behind)
    carry[0] = x0
    carry[1] = y0
    w = edge[1, block]
    gr = gsum[0] + x0 * w
    gl = gsum[1] + x0 * moment[1] + xm * w + moment[0] * y0
    totals[0, :, fl] = totals[0, :, fl] + scale * gr
    totals[1, :, fl] = totals[1, :, fl] - scale * (res[:, fl] * rate) * gl


def output_block(scale, fl, res, logr, conv, grad, xs, ys, carry, a_s, p_s, q_s):
    rows = conv.shape[0]
    modes = res.shape[0]
    segs = rows // SEG
    rate = jnp.exp(logr[:, fl])
    amp = res[:, fl] * scale
    a_s[...] = jnp.exp(-rate)
    seg_decay = jnp.exp(-rate * float(SEG))
    p = amp * carry[0]
    q = amp * carry[1]
    for seg in range(segs):
        at = slice(seg * modes, (seg + 1) * modes)
        p_s[at, :] = amp * xs[at, :] + p
        p = p * seg_decay
        back = segs - 1 - seg
        at = slice(back * modes, (back + 1) * modes)
        q_s[at, :] = amp * ys[at, :] + q
        q = q * seg_decay

    @pl.loop(0, segs // SUB)
    def _(group):
        base = group * (SUB * SEG)
        for half in range(0, modes, SUB):
            decay = [spread(a_s, half + k) for k in range(SUB)]
            p = [rows_of(p_s, group * (SUB * modes) + half + k, modes) for k in range(SUB)]
            q = [rows_of(q_s, group * (SUB * modes) + half + k, modes) for k in range(SUB)]
            for j in range(SEG):
                at = pl.ds(base + j, SUB, stride=SEG)
                conv[at, :] = conv[at, :] + tree(p)
                q = [decay[k] * q[k] for k in range(SUB)]
                at = pl.ds(base + SEG - 1 - j, SUB, stride=SEG)
                grad[at, :] = grad[at, :] + tree(q)
                if j < SEG - 1:
                    p = [decay[k] * p[k] for k in range(SUB)]


def whole_kernel(
    scale, norm, parts, groups_chan,
    sig_h, gate_h, outer_h, cot_h, res_h, logr_h,
    out_sig_h, out_gate_h, out_outer_h, sums_h,
    ins, params, outs, g_s, w_s, conv, grad, xs, ys, edge, edges, moment, gsum, carry, h_s,
    a_s, pw_s, st, lag_s, p_s, q_s, totals, pieces, landed, slots, final,
    in_sem, param_sem, out_sem, edge_send, edge_recv, rs_send, rs_recv, mid_send, mid_recv, end_send, end_recv,
):
    rows, cols = sig_h.shape
    modes, filters = res_h.shape
    blocks = cols // LANES
    place = lax.axis_index("seq")
    column = lax.axis_index("chan")
    pairs = pair_size(groups_chan)
    barrier = pltpu.get_barrier_semaphore()

    def remote(src, dst, send, recv, device):
        return pltpu.make_async_remote_copy(
            src_ref=src, dst_ref=dst, send_sem=send, recv_sem=recv, device_id=device, device_id_type=MESH
        )

    low = lax.rem(column, pairs)
    high = column // pairs
    upper = groups_chan // pairs
    team = parts * pairs
    member = place * pairs + low

    def mate(index):
        return {"seq": index // pairs, "chan": high * pairs + lax.rem(index, pairs)}

    def tower(index):
        return {"chan": index * pairs + low}

    for d in range(1, team):
        pl.semaphore_signal(barrier, inc=1, device_id=mate(lax.rem(member + d, team)), device_id_type=MESH)
    for d in range(1, upper):
        pl.semaphore_signal(barrier, inc=1, device_id=tower(lax.rem(high + d, upper)), device_id_type=MESH)

    param_copies = [
        pltpu.make_async_copy(ref, params.at[i], param_sem.at[i]) for i, ref in enumerate((res_h, logr_h))
    ]
    for copy in param_copies:
        copy.start()

    def fetch(i, ref, block):
        return pltpu.make_async_copy(ref.at[:, block_lanes(block)], ins.at[i, block], in_sem.at[i, block])

    whole_inputs = (sig_h, gate_h, outer_h, cot_h)

    @pl.loop(0, blocks)
    def _(block):
        for i, ref in enumerate(whole_inputs):
            fetch(i, ref, block).start()

    for copy in param_copies:
        copy.wait()
    pl.semaphore_wait(barrier, team - 1 + upper - 1)
    res, logr = params.at[0], params.at[1]

    def edge_copy(d, block):
        other = lax.rem(place + d, parts)
        which = jnp.where(other > place, 0, 1)
        if block is None:
            src, dst = edge.at[which], edges.at[place]
        else:
            src, dst = edge.at[which, block], edges.at[place, block]
        return remote(src, dst, edge_send.at[d], edge_recv.at[d], {"seq": other})

    @pl.loop(0, blocks)
    def _(block):
        for i, ref in enumerate(whole_inputs):
            fetch(i, ref, block).wait()
        sig, gate, outer, cot = (ins.at[i, block] for i in range(4))
        state_block(
            scale, block, filter_lanes(block, cols, filters), sig, gate, outer, cot, res, logr,
            g_s.at[block], w_s.at[block], a_s, h_s.at[block], pw_s, st, lag_s, xs.at[block], ys.at[block], edge,
            moment.at[block], gsum.at[block],
        )
        for d in range(1, parts):
            edge_copy(d, block).start()

    def inner(first, last):
        @pl.loop(first, last)
        def _(block):
            inner_block(rows, g_s.at[block], w_s.at[block], h_s.at[block], conv.at[block], grad.at[block])

    early = (blocks + 1) // 2
    inner(0, early)
    for d in range(1, parts):
        source = lax.rem(place + parts - d, parts)
        remote(edge.at[0], edges.at[source], edge_send.at[d], edge_recv.at[d], {"seq": source}).wait_recv()
    totals[...] = jnp.zeros_like(totals)
    edges[place] = jnp.zeros_like(edge[0])

    @pl.loop(0, blocks)
    def _(block):
        gradient_block(
            scale, parts, rows, block, filter_lanes(block, cols, filters), edges, edge, moment.at[block],
            gsum.at[block], res, logr, totals, carry.at[block],
        )

    size = 2 * modes // team
    for p in range(team):
        which, first = divmod(p * size, modes)
        pieces[p] = totals[which, first : first + size, :]

    def scatter(d):
        other = lax.rem(member + d, team)
        return remote(pieces.at[other], landed.at[d], rs_send.at[d], rs_recv.at[d], mate(other))

    def middle(d, back=False):
        other = lax.rem(high + (upper - d if back else d), upper)
        slot = slots.at[other if back else high]
        return remote(slot, slot, mid_send.at[d], mid_recv.at[d], tower(other))

    def ending(d, back=False):
        other = lax.rem(member + (team - d if back else d), team)
        slot = final.at[other if back else member]
        return remote(slot, slot, end_send.at[d], end_recv.at[d], mate(other))

    for d in range(1, team):
        scatter(d).start()
    inner(early, blocks)

    def put(i, block):
        target = (out_sig_h, out_gate_h, out_outer_h)[i]
        return pltpu.make_async_copy(outs.at[i, block], target.at[:, block_lanes(block)], out_sem.at[i, block])

    def outputs(first, last):
        if first == last:
            return

        @pl.loop(first, last)
        def _(block):
            output_block(
                scale, filter_lanes(block, cols, filters), res, logr, conv.at[block], grad.at[block], xs.at[block],
                ys.at[block], carry.at[block], a_s, p_s, q_s,
            )
            d = grad[block]
            outs[0, block] = (d * ins[1, block].astype(f32)).astype(jnp.bfloat16)
            outs[1, block] = (d * ins[0, block].astype(f32)).astype(jnp.bfloat16)
            outs[2, block] = (conv[block] * ins[3, block].astype(f32)).astype(jnp.bfloat16)
            for i in range(3):
                put(i, block).start()

    first_stop = blocks // 8
    second_stop = blocks - blocks // 4
    outputs(0, first_stop)
    for d in range(1, team):
        scatter(d).wait_recv()
    mine = pieces[member]
    for d in range(1, team):
        mine = mine + landed[d]
    slots[high] = mine
    for d in range(1, upper):
        middle(d).start()
    outputs(first_stop, second_stop)
    for d in range(1, upper):
        middle(d, back=True).wait_recv()
    summed = slots[0]
    for other in range(1, upper):
        summed = summed + slots[other]
    final[member] = norm * summed
    for d in range(1, team):
        ending(d).start()
    outputs(second_stop, blocks)
    for d in range(1, team):
        ending(d, back=True).wait_recv()
    for p in range(team):
        which, first = divmod(p * size, modes)
        sums_h[which, first : first + size, :] = final[p]

    for d in range(1, parts):
        edge_copy(d, None).wait_send()
    for d in range(1, team):
        scatter(d).wait_send()
        ending(d).wait_send()
    for d in range(1, upper):
        middle(d).wait_send()

    @pl.loop(0, blocks)
    def _(block):
        for i in range(3):
            put(i, block).wait()


def pass_kernel(sig, gate, outer, sums, out_sig, out_gate, out_outer, out_res, out_rate, held, sums_held, sem_in, sem_out):
    chunks, depth = held.shape[1:3]
    todo = []
    for i, (src, dst) in enumerate(((sig, out_sig), (gate, out_gate), (outer, out_outer))):
        for c in range(chunks):
            at = pl.ds(c * depth, depth)
            todo.append((src.at[at, :], held.at[i, c], dst.at[at, :]))
    for i, dst in enumerate((out_res, out_rate)):
        todo.append((sums.at[i], sums_held.at[i], dst))
    into = [pltpu.make_async_copy(src, mid, sem_in.at[n]) for n, (src, mid, _) in enumerate(todo)]
    out = [pltpu.make_async_copy(mid, dst, sem_out.at[n]) for n, (_, mid, dst) in enumerate(todo)]
    for copy in into:
        copy.start()
    for first, second in zip(into, out):
        first.wait()
        second.start()
    for copy in out:
        copy.wait()


def pair_size(columns):
    return 2 if columns % 2 == 0 else 1


def on_device(signal_in, gate_in, outer_gate, cotangent, residues, log_rates):
    parts = lax.axis_size("seq")
    groups_chan = lax.axis_size("chan")
    rows, cols = signal_in.shape
    modes, filters = residues.shape
    total = parts * rows
    blocks = cols // LANES
    segs = rows // SEG
    groups = segs // SUB
    pairs = pair_size(groups_chan)
    team = parts * pairs
    upper = groups_chan // pairs
    size = 2 * modes // team
    scale = float(total) ** (-0.5)
    norm = float(total * cols * groups_chan // filters) ** (-0.5)
    whole = pl.BlockSpec(memory_space=pltpu.VMEM)
    far = pl.BlockSpec(memory_space=pl.ANY)
    shape = jax.ShapeDtypeStruct
    small = pltpu.VMEM((modes, LANES), f32)
    tiles = pltpu.VMEM((blocks, rows, LANES), f32)
    states = pltpu.VMEM((blocks, segs * modes, LANES), f32)
    pair = pltpu.VMEM((blocks, 2, modes, LANES), f32)
    dma = pltpu.SemaphoreType.DMA
    narrow = shape((rows, cols), jnp.bfloat16)
    *products, sums = pl.pallas_call(
        functools.partial(whole_kernel, scale, norm, parts, groups_chan),
        out_shape=(
            narrow,
            narrow,
            narrow,
            shape((2, modes, filters), f32),
        ),
        in_specs=[pl.BlockSpec(memory_space=pltpu.HBM)] * 6,
        out_specs=(far, far, far, whole),
        scratch_shapes=[
            pltpu.VMEM((4, blocks, rows, LANES), jnp.bfloat16),
            pltpu.VMEM((2, modes, filters), f32),
            pltpu.VMEM((3, blocks, rows, LANES), jnp.bfloat16),
            tiles,
            tiles,
            tiles,
            tiles,
            states,
            states,
            pltpu.VMEM((2, blocks, modes, LANES), f32),
            pltpu.VMEM((parts, blocks, modes, LANES), f32),
            pair,
            pair,
            pair,
            pltpu.VMEM((blocks, SEG, LANES), f32),
            small,
            pltpu.VMEM((SEG * modes, LANES), f32),
            pltpu.VMEM((4, modes * segs, LANES), f32),
            pltpu.VMEM((groups * SEG * SUB, LANES), f32),
            pltpu.VMEM((segs * modes, LANES), f32),
            pltpu.VMEM((segs * modes, LANES), f32),
            pltpu.VMEM((2, modes, filters), f32),
            pltpu.VMEM((team, size, filters), f32),
            pltpu.VMEM((team, size, filters), f32),
            pltpu.VMEM((upper, size, filters), f32),
            pltpu.VMEM((team, size, filters), f32),
            dma((4, blocks)),
            dma((2,)),
            dma((3, blocks)),
            dma((parts,)),
            dma((parts,)),
            dma((team,)),
            dma((team,)),
            dma((upper,)),
            dma((upper,)),
            dma((team,)),
            dma((team,)),
        ],
        compiler_params=pltpu.CompilerParams(
            collective_id=0, has_side_effects=True
        ),
        name="whole",
    )(signal_in, gate_in, outer_gate, cotangent, residues, log_rates)
    chunks = 2
    return pl.pallas_call(
        pass_kernel,
        out_shape=(narrow, narrow, narrow, shape((modes, filters), f32), shape((modes, filters), f32)),
        in_specs=[far] * 4,
        out_specs=(far,) * 5,
        scratch_shapes=[
            pltpu.VMEM((3, chunks, rows // chunks, cols), jnp.bfloat16),
            pltpu.VMEM((2, modes, filters), f32),
            dma((3 * chunks + 2,)),
            dma((3 * chunks + 2,)),
        ],
        name="passed",
    )(*products, sums)


def solution(mesh):
    placed = (P("seq", "chan"), P("seq", "chan"), P("seq", "chan"), P("seq", "chan"), P(), P())
    return jax.shard_map(
        on_device,
        mesh=mesh,
        in_specs=placed,
        out_specs=(P("seq", "chan"), P("seq", "chan"), P("seq", "chan"), P(), P()),
        check_vma=False,
    )
```
